32 devices in a mesh: dp: 8 (over y, x, core), mp: 4 (over z).
Axes of the slice: x: 2, y: 2, z: 4, core: 2. Of those that a mesh axis runs over, the one named last changes fastest.
Arguments:
- tokens: bfloat16 [16384, 768], P(('dp', 'mp')), may hold values from -6 to 6
- timesteps: int32 [16], P('dp'), may hold values from 0 to 999
- masked: int32 [16384], P(('dp', 'mp')), may hold values from 0 to 1, as said below
- cotangent: bfloat16 [16384, 768], P(('dp', 'mp')), may hold values from -6 to 6
- step_table: bfloat16 [1000, 768], replicated, may hold values from -3 to 3
- qkv_weight: bfloat16 [768, 3, 768], P(None, None, 'mp'), may hold values from -0.21875 to 0.21875
- qv_bias: float32 [2, 768], P(None, 'mp'), may hold values from -0.6 to 0.6
- out_weight: bfloat16 [768, 768], P('mp'), may hold values from -3.5 to 3.5
- out_bias: float32 [768], replicated, may hold values from -1.8 to 1.8
- first_gain: float32 [768], replicated, may hold values from 0.5 to 1.5
- first_shift: float32 [768], replicated, may hold values from -0.6 to 0.6
- second_gain: float32 [768], replicated, may hold values from 0.5 to 1.5
- second_shift: float32 [768], replicated, may hold values from -0.6 to 0.6
- in_weight: bfloat16 [768, 3072], P(None, 'mp'), may hold values from -0.21875 to 0.21875
- in_bias: bfloat16 [3072], P('mp'), may hold values from -1.796875 to 1.796875
- back_weight: bfloat16 [3072, 768], P('mp'), may hold values from -0.109375 to 0.109375
- back_bias: float32 [768], replicated, may hold values from -1.8 to 1.8
Outputs:
- output: bfloat16 [16384, 768], P(('dp', 'mp'))
- input_grad: float32 [16384, 768], P(('dp', 'mp'))
- table_grad: float32 [1000, 768], replicated
- qkv_weight_grad: float32 [768, 3, 768], P(None, None, 'mp')
- qv_bias_grad: float32 [2, 768], P(None, 'mp')
- out_weight_grad: float32 [768, 768], P('mp')
- out_bias_grad: float32 [768], replicated
- first_gain_grad: float32 [768], replicated
- first_shift_grad: float32 [768], replicated
- second_gain_grad: float32 [768], replicated
- second_shift_grad: float32 [768], replicated
- in_weight_grad: float32 [768, 3072], P(None, 'mp')
- in_bias_grad: float32 [3072], P('mp')
- back_weight_grad: float32 [3072, 768], P('mp')
- back_bias_grad: float32 [768], replicated
The draws below stay inside these ranges and needn't reach their ends.
Inputs may be any that keep to these rules, and one draw needn't show every extreme that they name: 1 marks a masked token; all tokens of one sequence share one chance of being masked.
All inputs are finite; a program needn't handle non-finite values.
Results may differ from the reference program's by a relative error of at most 0.012.
The reference program's roundings to bfloat16 on the way count: a program that leaves them out, or rounds other values in their place, can miss the bound.
Values may be sent and summed in bfloat16 or wider, within the bound.
A program may use at most 128 MiB of HBM per device.

```python
import jax
import jax.numpy as jnp
from jax import lax

D = 768
HEADS = 12
HEAD_DIM = 64
FF = 3072
NSTEPS = 1000
L = 1024
SEQ_DEV = 2
SEQS = 16
TOKENS = 16384
N_DP = 8


def draw_masked(key, part):
    level_key = jax.random.fold_in(key, 11)
    toss_key = jax.random.fold_in(key, 12)
    levels = jax.random.randint(level_key, (SEQS, 1), 0, 4)
    chance = jnp.left_shift(jnp.full((SEQS, 1), 8, jnp.int32), levels)
    tosses = jax.random.randint(toss_key, (SEQS, L), 0, 64)
    return (tosses < chance).astype(jnp.int32).reshape(SEQS * L)


def place_ends(values, key, low, high):
    longest = values.shape.index(max(values.shape))
    spots = []
    for shift in (0, 1):
        where = [jax.random.randint(jax.random.fold_in(key, axis), (), 0, length) for axis, length in enumerate(values.shape)]
        where[longest] = (where[longest] + shift) % values.shape[longest]
        spots.append(tuple(where))
    return values.at[spots[0]].set(low).at[spots[1]].set(high)


def level_of(own_key, dims, pieces, smallest, largest):
    def one(axis_at, blocks):
        heights = jax.random.uniform(jax.random.fold_in(jax.random.fold_in(own_key, 6), axis_at), (blocks,), jnp.float32, smallest / len(pieces), largest / len(pieces))
        return jnp.repeat(jnp.exp(heights), dims[axis_at] // blocks).reshape((-1,) + (1,) * (len(dims) - axis_at - 1))

    level = one(*pieces[0])
    for cut in pieces[1:]:
        level = level * one(*cut)
    return level


def gaussian(own_key, extent, scale, limit, split=(), held_as=jnp.bfloat16):
    loudness = level_of(own_key, extent, split, -0.22, 0.18) if split else 1.0
    values = jax.random.normal(own_key, extent, jnp.float32) * scale * loudness
    return jnp.minimum(jnp.maximum(values, -limit), limit).astype(held_as)


def setup_inputs(seed: int = 0) -> dict:
    streams_of = jax.random.split(jax.random.key(seed), 18)
    tokens = gaussian(streams_of[0], (TOKENS, D), 1.0, 6.0, ((0, 32),))
    timesteps = place_ends(jax.random.randint(streams_of[1], (SEQS,), 0, NSTEPS), jax.random.fold_in(streams_of[1], 1), 0, NSTEPS - 1).astype(jnp.int32)
    masked = draw_masked(jax.random.fold_in(streams_of[17], 71), 0)
    cotangent = gaussian(streams_of[3], (TOKENS, D), 1.0, 6.0, ((0, 32),))
    step_table = gaussian(streams_of[4], (NSTEPS, D), 0.5, 3.0)
    qkv_weight = gaussian(streams_of[5], (D, 3, D), D ** -0.5, 0.21875, ((2, 4),))
    qv_bias = gaussian(streams_of[6], (2, D), 0.1, 0.6, ((1, 4),), jnp.float32)
    out_weight = gaussian(streams_of[7], (D, D), (4 * D // L) ** -0.5, 3.5, ((0, 4),))
    out_bias = gaussian(streams_of[8], (D,), 0.3, 1.8, (), jnp.float32)
    first_gain = jnp.clip(1.0 + 0.1 * jax.random.normal(streams_of[9], (D,), jnp.float32), 0.5, 1.5)
    first_shift = gaussian(streams_of[10], (D,), 0.1, 0.6, (), jnp.float32)
    second_gain = jnp.clip(1.0 + 0.1 * jax.random.normal(streams_of[11], (D,), jnp.float32), 0.5, 1.5)
    second_shift = gaussian(streams_of[12], (D,), 0.1, 0.6, (), jnp.float32)
    in_weight = gaussian(streams_of[13], (D, FF), D ** -0.5, 0.21875, ((1, 4),))
    in_bias = gaussian(streams_of[14], (FF,), 0.3, 1.796875, ((0, 4),))
    back_weight = gaussian(streams_of[15], (FF, D), FF ** -0.5, 0.109375, ((0, 4),))
    back_bias = gaussian(streams_of[16], (D,), 0.3, 1.8, (), jnp.float32)
    return dict(tokens=tokens, timesteps=timesteps, masked=masked, cotangent=cotangent, step_table=step_table, qkv_weight=qkv_weight, qv_bias=qv_bias, out_weight=out_weight, out_bias=out_bias, first_gain=first_gain, first_shift=first_shift, second_gain=second_gain, second_shift=second_shift, in_weight=in_weight, in_bias=in_bias, back_weight=back_weight, back_bias=back_bias)


EPSILON = 1e-05
HIGHEST = lax.Precision.HIGHEST

@jax.custom_vjp
def low(v):
    return lax.optimization_barrier(v.astype(jnp.bfloat16)).astype(jnp.float32)

@jax.custom_vjp
def low_back(v):
    return v

def low_keep(v):
    return (low(v), None)

def low_pass(kept, grad):
    return (grad,)

def back_keep(v):
    return (v, None)

def back_low(kept, grad):
    return (low(grad),)
low.defvjp(low_keep, low_pass)
low_back.defvjp(back_keep, back_low)

def layer_norm(values, gain, shift):
    center = values - lax.optimization_barrier(jnp.mean(values, axis=-1, keepdims=True))
    scaled = center * lax.rsqrt(lax.optimization_barrier(jnp.mean(center * center, axis=-1, keepdims=True)) + EPSILON)
    return scaled * gain + shift

def forward(rows_in, params, tok_steps):
    step_table, qkv_weight, qv_bias, out_weight, out_bias, first_gain, first_shift, second_gain, second_shift, in_weight, in_bias, back_weight, back_bias = params
    stream = rows_in + step_table[tok_steps]
    normed_one = low(layer_norm(stream, first_gain, first_shift))
    projected = jnp.einsum('rd,djc->rjc', normed_one, qkv_weight, precision=HIGHEST)
    qkv_bias = jnp.stack([qv_bias[0], jnp.zeros_like(qv_bias[0]), qv_bias[1]])
    projected = low_back(low(projected + qkv_bias))
    heads = projected.reshape(SEQ_DEV, L, 3, HEADS, HEAD_DIM)
    query_heads = heads[:, :, 0]
    key_heads = heads[:, :, 1]
    value_heads = heads[:, :, 2]
    scores = low_back(jnp.einsum('bqhc,bkhc->bhqk', query_heads, key_heads, precision=HIGHEST) * HEAD_DIM ** (-0.5))
    attn_probs = low(jax.nn.softmax(scores, axis=-1))
    attended = jnp.einsum('bhqk,bkhc->bqhc', attn_probs, value_heads, precision=HIGHEST).reshape(SEQ_DEV * L, D)
    attended = low_back(low(attended))
    branch = low_back(jnp.dot(attended, out_weight, precision=HIGHEST) + out_bias)
    mid_stream = stream + branch
    normed_two = low(layer_norm(mid_stream, second_gain, second_shift))
    preact = low_back(jnp.dot(normed_two, in_weight, precision=HIGHEST) + in_bias)
    active = low(jax.nn.gelu(preact))
    feed_out = low_back(jnp.dot(active, back_weight, precision=HIGHEST) + back_bias)
    return mid_stream + feed_out

def reference(tokens, timesteps, masked, cotangent, step_table, qkv_weight, qv_bias, out_weight, out_bias, first_gain, first_shift, second_gain, second_shift, in_weight, in_bias, back_weight, back_bias):
    params = jax.tree.map(lambda member: member.astype(jnp.float32), (step_table, qkv_weight, qv_bias, out_weight, out_bias, first_gain, first_shift, second_gain, second_shift, in_weight, in_bias, back_weight, back_bias))
    group_rows = SEQ_DEV * L
    inputs_all = tokens.astype(jnp.float32).reshape(N_DP, group_rows, D)
    grads_all = (cotangent.astype(jnp.float32) * masked.astype(jnp.float32)[:, None]).reshape(N_DP, group_rows, D)
    steps_all = timesteps.reshape(N_DP, SEQ_DEV)

    def one_group(totals, group_item):
        group_in, group_cot, group_steps = group_item
        tok_steps = jnp.repeat(group_steps, L, total_repeat_length=group_rows)
        result, pullback = jax.vjp(lambda rows_in, members: forward(rows_in, members, tok_steps), group_in, params)
        input_part, param_parts = pullback(group_cot)
        totals = jax.tree.map(jnp.add, totals, param_parts)
        return (totals, (result.astype(jnp.bfloat16), input_part))
    zeros_all = jax.tree.map(jnp.zeros_like, params)
    totals, (outputs, input_parts) = lax.scan(one_group, zeros_all, (inputs_all, grads_all, steps_all))
    return (outputs.reshape(TOKENS, D), input_parts.reshape(TOKENS, D), totals[0], totals[1], totals[2], totals[3], totals[4], totals[5], totals[6], totals[7], totals[8], totals[9], totals[10], totals[11], totals[12])
```

```python
import functools

import jax
import jax.numpy as jnp
from jax import lax
from jax.experimental import pallas as pl
from jax.experimental.pallas import tpu as pltpu
from jax.sharding import Mesh, PartitionSpec as P

HEAD_DIM = 64
NSTEPS = 1000
L = 1024
EPSILON = 1e-05
HIGHEST = lax.Precision.HIGHEST
MESH = pl.DeviceIdType.MESH
BF = jnp.bfloat16
F32 = jnp.float32


def place():
    k = lax.axis_index("k")
    c = lax.axis_index("c")
    z = lax.axis_index("mp")
    return k, c, z


def flip(i, bit):
    if bit == 1:
        return i + 1 - 2 * lax.rem(i, 2)
    if bit == 2:
        return lax.rem(i + 2, 4)
    return 3 - i


def enter_barrier():
    k, c, z = place()
    sem = pltpu.get_barrier_semaphore()
    peers = [{"c": 1 - c}, {"k": flip(k, 1)}, {"k": flip(k, 2)}] + [{"mp": flip(z, r)} for r in (1, 2, 3)]
    peers.append({"c": 1 - c, "mp": flip(z, 1)})
    for peer in peers:
        pl.semaphore_signal(sem, inc=1, device_id=peer, device_id_type=MESH)
    pl.semaphore_wait(sem, len(peers))


def remote(src, dst, ss, rs, peer):
    return pltpu.make_async_remote_copy(src_ref=src, dst_ref=dst, send_sem=ss, recv_sem=rs, device_id=peer, device_id_type=MESH)


def cut(ref, lead, q, k, half, c):
    first, count = {None: (0, q), 0: (0, (q // 32) * 16 if q % 32 else q // 2), 1: ((q // 32) * 16 if q % 32 else q // 2, 0)}[half]
    if half == 1:
        count = q - first
    start = pl.multiple_of(k * q + first, 16)
    cols = pl.ds(pl.multiple_of(c * 384, 128), 384)
    return ref.at[lead + (slice(None), pl.ds(start, count), cols)]


def cols_of(ref, lead, c):
    return ref.at[lead + (slice(None), slice(None), pl.ds(pl.multiple_of(c * 384, 128), 384))]


def gather_kernel(qkv_ref, out_ref, in_ref, back_ref, bias_ref, tok_ref, grad_ref, row_ref,
                  wa, wm, bias, tok, grad, row, local_sem, ssem, rsem, bsem, brem, wsem, wrem):
    k, c, z = place()
    kx, ky = flip(k, 1), flip(k, 2)
    nx, ny, nc = {"k": kx}, {"k": ky}, {"c": 1 - c}
    locals_ = [
        (qkv_ref, wa.at[0, pl.ds(0, 3)]),
        (out_ref, wa.at[0, 3]),
        (in_ref, wm.at[0, 0]),
        (back_ref, wm.at[0, 1]),
        (bias_ref, bias.at[0]),
    ]
    copies = [pltpu.make_async_copy(s, d, local_sem.at[i]) for i, (s, d) in enumerate(locals_)]
    for cp in copies:
        cp.start()
    enter_barrier()
    stays = c == lax.rem(z, 2)
    swap_peer = {"c": 1 - c, "mp": flip(z, 1)}
    swaps = [(tok_ref, tok), (row_ref, row), (grad_ref, grad)]
    remote_swaps = [remote(s, d, wsem.at[i], wrem.at[i], swap_peer) for i, (s, d) in enumerate(swaps)]
    local_swaps = [pltpu.make_async_copy(s, d, local_sem.at[5 + i]) for i, (s, d) in enumerate(swaps)]

    @pl.when(stays)
    def _():
        for cp in local_swaps:
            cp.start()

    @pl.when(jnp.logical_not(stays))
    def _():
        for cp in remote_swaps:
            cp.start()

    for cp in copies:
        cp.wait()
    small = [remote(bias.at[0], bias.at[r], bsem.at[r - 1], brem.at[r - 1], {"mp": flip(z, r)}) for r in (1, 2, 3)]
    for cp in small:
        cp.start()
    chunks = [(wa, 48, 1), (wa, 48, 2), (wa, 48, 3), (wm, 192, 1), (wm, 192, 2), (wm, 192, 3)]

    def sends(i):
        w, q, r = chunks[i]
        at = lambda ref, slot, kk, half: cut(ref, (slot,), q, kk, half, c)
        stage0 = [remote(at(w, 0, k, None), at(w, r, k, None), ssem.at[i, 0], rsem.at[i, 0], {"mp": flip(z, r)})]
        stage1 = [
            remote(at(w, r, k, None), at(w, r, k, None), ssem.at[i, 1], rsem.at[i, 1], nx),
            remote(at(w, r, k, None), at(w, r, k, None), ssem.at[i, 2], rsem.at[i, 2], ny),
        ]
        stage2 = [
            remote(at(w, r, ky, 0), at(w, r, ky, 0), ssem.at[i, 3], rsem.at[i, 3], nx),
            remote(at(w, r, kx, 1), at(w, r, kx, 1), ssem.at[i, 4], rsem.at[i, 4], ny),
        ]
        stage3 = [remote(cols_of(w, (r,), c), cols_of(w, (r,), c), ssem.at[i, 5], rsem.at[i, 5], nc)]
        return [stage0, stage1, stage2, stage3]

    def lands(i):
        w, q, r = chunks[i]
        at = lambda ref, slot, kk, half: cut(ref, (slot,), q, kk, half, c)
        kd = flip(k, 3)
        return [
            [(at(w, r, k, None), rsem.at[i, 0])],
            [(at(w, r, kx, None), rsem.at[i, 1]), (at(w, r, ky, None), rsem.at[i, 2])],
            [(at(w, r, kd, 0), rsem.at[i, 3]), (at(w, r, kd, 1), rsem.at[i, 4])],
            [(cols_of(w, (r,), 1 - c), rsem.at[i, 5])],
        ]

    n = len(chunks)
    all_sends = [sends(i) for i in range(n)]
    all_lands = [lands(i) for i in range(n)]
    for i in range(n):
        for cp in all_sends[i][0]:
            cp.start()
    for step in range(n + 3):
        for stage in range(4):
            i = step - stage
            if 0 <= i < n:
                for ref, sem in all_lands[i][stage]:
                    pltpu.make_async_copy(ref, ref, sem).wait()
                if stage < 3:
                    for cp in all_sends[i][stage + 1]:
                        cp.start()
    for i in range(n):
        for stage in all_sends[i]:
            for cp in stage:
                cp.wait_send()
    for cp in small:
        cp.wait()

    @pl.when(stays)
    def _():
        for cp in local_swaps:
            cp.wait()

    @pl.when(jnp.logical_not(stays))
    def _():
        for cp in remote_swaps:
            cp.wait()


def gather_weights(qkv, out, win, back, bias, tok, grad, row):
    hbm = pl.BlockSpec(memory_space=pl.ANY)
    shapes = (
        jax.ShapeDtypeStruct((4, 4, 192, 768), BF),
        jax.ShapeDtypeStruct((4, 2, 768, 768), BF),
        jax.ShapeDtypeStruct((4, 8, 768), F32),
        jax.ShapeDtypeStruct((512, 768), BF),
        jax.ShapeDtypeStruct((512, 768), BF),
        jax.ShapeDtypeStruct((16, 768), BF),
    )
    dma = pltpu.SemaphoreType.DMA
    return pl.pallas_call(
        gather_kernel,
        out_shape=shapes,
        in_specs=[hbm] * 8,
        out_specs=[hbm] * 6,
        scratch_shapes=[dma((8,)), dma((6, 6)), dma((6, 6)), dma((3,)), dma((3,)), dma((3,)), dma((3,))],
        compiler_params=pltpu.CompilerParams(collective_id=0, has_side_effects=True),
        name="gather_weights",
    )(qkv, out, win, back, bias, tok, grad, row)


def reduce_kernel(ga_ref, gm_ref, small_ref, seq_ref, og_ref, oo_ref,
                  outa, outm, small_out, seq_out, og_out, oo_out,
                  ga, gm, cra, crm, raa, rba, ram, rbm, bxa, bya, bxm, bym, za, zm, fa, fm, hyper,
                  local_sem, ssem, rsem, fsem, frem, hsem, hrem, qsem, qrem, wsem, wrem):
    k, c, z = place()
    kx, ky, kd = flip(k, 1), flip(k, 2), flip(k, 3)
    nx, ny, nc = {"k": kx}, {"k": ky}, {"c": 1 - c}
    copies = [pltpu.make_async_copy(ga_ref, ga, local_sem.at[0]), pltpu.make_async_copy(gm_ref, gm, local_sem.at[1]),
              pltpu.make_async_copy(small_ref, hyper.at[0], local_sem.at[2])]
    me = k * 8 + c * 4 + z
    copies.append(pltpu.make_async_copy(seq_ref, seq_out.at[me], local_sem.at[3]))
    for cp in copies:
        cp.start()
    enter_barrier()
    for cp in copies:
        cp.wait()
    stays = c == lax.rem(z, 2)
    swap_peer = {"c": 1 - c, "mp": flip(z, 1)}
    swaps = [(og_ref, og_out), (oo_ref, oo_out)]
    remote_swaps = [remote(s, d, wsem.at[i], wrem.at[i], swap_peer) for i, (s, d) in enumerate(swaps)]
    local_swaps = [pltpu.make_async_copy(s, d, local_sem.at[4 + i]) for i, (s, d) in enumerate(swaps)]

    @pl.when(stays)
    def _():
        for cp in local_swaps:
            cp.start()

    @pl.when(jnp.logical_not(stays))
    def _():
        for cp in remote_swaps:
            cp.start()

    chunks = [(gm, crm, r, 1, 192, ram, rbm, bxm, bym, zm) for r in range(4)]
    chunks += [(ga, cra, 2 * h, 2, 48, raa, rba, bxa, bya, za) for h in range(2)]
    mine = pl.ds(pl.multiple_of(c * 384, 128), 384)
    other = pl.ds(pl.multiple_of((1 - c) * 384, 128), 384)

    def part(q, half):
        first = (q // 32) * 16 if q % 32 else q // 2
        return (0, q) if half is None else ((0, first) if half == 0 else (first, q - first))

    def rows(q, kk, half):
        first, count = part(q, half)
        return pl.ds(pl.multiple_of(kk * q + first, 16), count)

    def make(i):
        g, cr, s0, ns, q, ra, rb, bx, by, zz = chunks[i]
        ss = pl.ds(s0, ns)
        every = slice(None)
        st = {}
        st["core"] = [remote(g.at[ss, every, every, other], cr.at[ss], ssem.at[i, 0], rsem.at[i, 0], nc)]
        st["a"] = [
            remote(g.at[ss, every, rows(q, kd, 0), mine], ra.at[ss], ssem.at[i, 1], rsem.at[i, 1], nx),
            remote(g.at[ss, every, rows(q, kd, 1), mine], rb.at[ss], ssem.at[i, 2], rsem.at[i, 2], ny),
        ]
        st["b"] = [
            remote(g.at[ss, every, rows(q, kx, None), mine], bx.at[ss], ssem.at[i, 3], rsem.at[i, 3], nx),
            remote(g.at[ss, every, rows(q, ky, None), mine], by.at[ss], ssem.at[i, 4], rsem.at[i, 4], ny),
        ]
        st["z"] = [
            remote(g.at[r, every, rows(q, k, None), mine], zz.at[r - 1], ssem.at[i, 4 + r], rsem.at[i, 4 + r], {"mp": flip(z, r)})
            for r in range(max(s0, 1), s0 + ns)
        ]
        return st

    all_sends = [make(i) for i in range(len(chunks))]

    def start(cps):
        for cp in cps:
            cp.start()

    def got(cps):
        for cp in cps:
            cp.wait_recv()

    def add_into(dst, pieces):
        n, m = dst.shape[0], dst.shape[1]
        for a in range(n):
            for b in range(m):
                total = dst[a, b].astype(F32)
                for p in pieces:
                    total = total + p[a, b].astype(F32)
                dst[a, b] = total.astype(BF)

    def core_add(i):
        g, cr, s0, ns, q, *_ = chunks[i]

        @pl.loop(0, 4)
        def _(j):
            r = pl.ds(pl.multiple_of(j * q, 16), q)
            add_into(g.at[pl.ds(s0, ns), :, r, mine], [cr.at[pl.ds(s0, ns), :, r]])

    def a_add(i):
        g, cr, s0, ns, q, ra, rb, *_ = chunks[i]
        ss = pl.ds(s0, ns)
        add_into(g.at[ss, :, rows(q, ky, 0), mine], [ra.at[ss]])
        add_into(g.at[ss, :, rows(q, kx, 1), mine], [rb.at[ss]])

    def b_add(i):
        g, cr, s0, ns, q, ra, rb, bx, by, zz = chunks[i]
        ss = pl.ds(s0, ns)
        add_into(g.at[ss, :, rows(q, k, None), mine], [bx.at[ss], by.at[ss]])

    steps = [
        (lambda i: None, "core"),
        (core_add, "a"),
        (a_add, "b"),
        (b_add, "z"),
    ]
    names = ["core", "a", "b", "z"]
    n = len(chunks)
    for step in range(n + 4):
        for stage in range(5):
            i = step - stage
            if 0 <= i < n:
                if stage > 0:
                    got(all_sends[i][names[stage - 1]])
                if stage < 4:
                    steps[stage][0](i)
                    start(all_sends[i][names[stage]])
    finals = [(gm, zm, fm, 192, 0), (ga, za, fa, 48, 1)]
    gathers = []
    for g, zz, f, q, j in finals:
        m = g.shape[1]
        for b in range(m):
            total = g[0, b, rows(q, k, None), mine].astype(F32)
            for r in range(3):
                total = total + zz[r, b].astype(F32)
            f[b, rows(q, k, None), mine] = total.astype(BF)
        at = lambda kk, half: f.at[:, rows(q, kk, half), mine]
        g1 = [remote(at(k, None), at(k, None), fsem.at[j, 0], frem.at[j, 0], nx),
              remote(at(k, None), at(k, None), fsem.at[j, 1], frem.at[j, 1], ny)]
        g2 = [remote(at(ky, 0), at(ky, 0), fsem.at[j, 2], frem.at[j, 2], nx),
              remote(at(kx, 1), at(kx, 1), fsem.at[j, 3], frem.at[j, 3], ny)]
        g3 = [remote(f.at[:, :, mine], f.at[:, :, mine], fsem.at[j, 4], frem.at[j, 4], nc)]
        start(g1)
        gathers.append((g1, g2, g3))
    peers = [nc, nx, ny, {"mp": flip(z, 1)}, {"mp": flip(z, 2)}]
    hops = []
    seqs = []
    spans = [
        lambda kk, cc, zz_: (pl.ds(kk * 8 + cc * 4 + zz_, 1),),
    ]
    for t, peer in enumerate(peers):
        cp = remote(hyper.at[2 * t], hyper.at[2 * t + 1], hsem.at[t], hrem.at[t], peer)
        cp.start()
        hops.append(cp)
        if t < 2:
            for g1, g2, g3 in gathers:
                got([g1, g2][t])
                start([g2, g3][t])
        cp.wait_recv()
        hyper[2 * t + 2] = hyper[2 * t] + hyper[2 * t + 1]
    done = pltpu.make_async_copy(hyper.at[10], small_out, local_sem.at[6])
    done.start()
    zs = [remote(seq_ref, seq_out.at[me], qsem.at[r - 1], qrem.at[r - 1], {"mp": flip(z, r)}) for r in (1, 2, 3)]
    start(zs)
    got(zs)
    line = lambda kk, cc: seq_out.at[pl.ds(kk * 8 + cc * 4, 4)]
    c1 = [remote(line(k, c), line(k, c), qsem.at[3], qrem.at[3], nc)]
    start(c1)
    got(c1)
    chip = lambda kk: seq_out.at[pl.ds(kk * 8, 8)]
    x1 = [remote(chip(k), chip(k), qsem.at[4], qrem.at[4], nx), remote(chip(k), chip(k), qsem.at[5], qrem.at[5], ny)]
    start(x1)
    got(x1)
    x2 = [remote(chip(ky), chip(ky), qsem.at[6], qrem.at[6], nx)]
    start(x2)
    got(x2)
    for g1, g2, g3 in gathers:
        got(g3)
    outs = [pltpu.make_async_copy(fa, outa, local_sem.at[7]), pltpu.make_async_copy(fm, outm, local_sem.at[8])]
    start(outs)
    for cp in zs + c1 + x1 + x2 + hops:
        cp.wait_send()
    for g in gathers:
        for stage in g:
            for cp in stage:
                cp.wait_send()
    for st in all_sends:
        for stage in st.values():
            for cp in stage:
                cp.wait_send()
    for cp in outs + [done]:
        cp.wait()

    @pl.when(stays)
    def _():
        for cp in local_swaps:
            cp.wait()

    @pl.when(jnp.logical_not(stays))
    def _():
        for cp in remote_swaps:
            cp.wait()


def reduce_grads(ga, gm, small, seq, og, oo):
    hbm = pl.BlockSpec(memory_space=pl.ANY)
    dma = pltpu.SemaphoreType.DMA
    vm = pltpu.VMEM
    shapes = (
        jax.ShapeDtypeStruct((4, 192, 768), BF),
        jax.ShapeDtypeStruct((2, 768, 768), BF),
        jax.ShapeDtypeStruct(small.shape, F32),
        jax.ShapeDtypeStruct((32,) + seq.shape, F32),
        jax.ShapeDtypeStruct(og.shape, F32),
        jax.ShapeDtypeStruct(oo.shape, BF),
    )
    scratch = [
        vm((4, 4, 192, 768), BF),
        vm((4, 2, 768, 768), BF),
        vm((4, 4, 192, 384), BF),
        vm((4, 2, 768, 384), BF),
        vm((4, 4, 16, 384), BF),
        vm((4, 4, 32, 384), BF),
        vm((4, 2, 96, 384), BF),
        vm((4, 2, 96, 384), BF),
        vm((4, 4, 48, 384), BF),
        vm((4, 4, 48, 384), BF),
        vm((4, 2, 192, 384), BF),
        vm((4, 2, 192, 384), BF),
        vm((3, 4, 48, 384), BF),
        vm((3, 2, 192, 384), BF),
        vm((4, 192, 768), BF),
        vm((2, 768, 768), BF),
        vm((11,) + small.shape, F32),
        dma((9,)), dma((6, 8)), dma((6, 8)), dma((2, 5)), dma((2, 5)), dma((5,)), dma((5,)), dma((7,)), dma((7,)), dma((2,)), dma((2,)),
    ]
    return pl.pallas_call(
        reduce_kernel,
        out_shape=shapes,
        in_specs=[hbm] * 6,
        out_specs=[hbm] * 6,
        scratch_shapes=scratch,
        compiler_params=pltpu.CompilerParams(collective_id=1, has_side_effects=True, vmem_limit_bytes=60 << 20),
        name="reduce_grads",
    )(ga, gm, small, seq, og, oo)


def norm_parts(values):
    center = values - jnp.mean(values, axis=-1, keepdims=True)
    inverse = lax.rsqrt(jnp.mean(center * center, axis=-1, keepdims=True) + EPSILON)
    return (center * inverse, inverse)


def norm_back(upstream, normal, inverse):
    return inverse * (
        upstream
        - jnp.mean(upstream, axis=-1, keepdims=True)
        - normal * jnp.mean(upstream * normal, axis=-1, keepdims=True)
    )


def dots(spec, a, b):
    return jnp.einsum(spec, a, b, preferred_element_type=F32)


def shards(tokens, timesteps, masked, cotangent, step_table, qkv_weight, qv_bias, out_weight, out_bias,
           first_gain, first_shift, second_gain, second_shift, in_weight, in_bias, back_weight, back_bias):
    z = lax.axis_index("mp")
    c = lax.axis_index("c")
    seq = z // 2
    step = lax.dynamic_index_in_dim(timesteps, seq, keepdims=False)
    row = lax.dynamic_slice_in_dim(step_table, step, 1, axis=0)
    row16 = jnp.broadcast_to(row, (16, 768))
    grad_low = cotangent * masked.astype(BF)[:, None]
    bias = jnp.zeros((8, 768), F32).at[0].set(in_bias.astype(F32)).at[1, :192].set(qv_bias[0]).at[2, :192].set(qv_bias[1])
    wa, wm, biases, tok, grad, row_in = gather_weights(
        qkv_weight.transpose(1, 2, 0), out_weight, in_weight, back_weight, bias, tokens, grad_low, row16)
    stream = tok.astype(F32) + row_in[:1].astype(F32)
    first_hat, first_inv = norm_parts(stream)
    normed_one = (first_hat * first_gain + first_shift).astype(BF)
    qkv_bias = jnp.stack([biases[:, 1, :192], jnp.zeros((4, 192), F32), biases[:, 2, :192]], axis=1)
    proj = (dots("rd,spcd->rspc", normed_one, wa[:, :3]) + qkv_bias).astype(BF)
    heads = proj.reshape(512, 4, 3, 3, 64)
    q = heads[:, :, 0].reshape(512, 12, 64)
    kv = lax.all_gather(heads[:, :, 1:], "c", axis=0, tiled=True)
    keys = kv[:, :, 0].reshape(1024, 12, 64)
    vals = kv[:, :, 1].reshape(1024, 12, 64)
    scale = HEAD_DIM ** (-0.5)
    s = dots("qhc,khc->hqk", q, keys) * scale
    probs = jax.nn.softmax(s, axis=-1)
    low_probs = probs.astype(BF)
    attended = dots("hqk,khc->qhc", low_probs, vals).astype(BF).reshape(512, 768)
    wo = wa[:, 3].reshape(768, 768)
    branch = dots("rc,cd->rd", attended, wo)
    mid = stream + (branch + out_bias)
    second_hat, second_inv = norm_parts(mid)
    normed_two = (second_hat * second_gain + second_shift).astype(BF)
    grad_out = grad.astype(F32)
    preact = dots("rd,sdh->srh", normed_two, wm[:, 0]) + biases[:, 0][:, None, :]
    active = jax.nn.gelu(preact).astype(BF)
    feed = dots("srh,shd->rd", active, wm[:, 1])
    output = (mid + (feed + back_bias)).astype(BF)
    back_g = dots("srh,rd->shd", active, grad).astype(BF)
    pullback = jax.vjp(jax.nn.gelu, preact)[1]
    pre_grad = pullback(dots("rd,shd->srh", grad, wm[:, 1]))[0].astype(BF)
    in_bias_g = jnp.sum(pre_grad.astype(F32), axis=1)
    in_g = dots("rd,srh->sdh", normed_two, pre_grad).astype(BF)
    second_grad = dots("srh,sdh->rd", pre_grad, wm[:, 0])
    back_bias_g = jnp.sum(grad_out, axis=0)
    second_gain_g = jnp.sum(second_grad * second_hat, axis=0)
    second_shift_g = jnp.sum(second_grad, axis=0)
    mid_grad = grad_out + norm_back(second_grad * second_gain, second_hat, second_inv)
    branch_low = mid_grad.astype(BF)
    out_bias_g = jnp.sum(branch_low.astype(F32), axis=0)
    out_g = dots("rc,rd->cd", attended, branch_low).astype(BF).reshape(4, 192, 768)
    att_grad = dots("rd,cd->rc", branch_low, wo).astype(BF).reshape(512, 12, 64)
    dval = dots("hqk,qhc->khc", low_probs, att_grad)
    dprob = dots("qhc,khc->hqk", att_grad, vals)
    ds = (probs * (dprob - jnp.sum(dprob * probs, axis=-1, keepdims=True))).astype(BF)
    dq = (dots("hqk,khc->qhc", ds, keys) * scale).astype(BF)
    dk = dots("hqk,qhc->khc", ds, q) * scale
    dkv = lax.psum_scatter(jnp.stack([dk, dval], axis=1), "c", scatter_dimension=0, tiled=True).astype(BF)
    qkv_g = jnp.stack([dq, dkv[:, 0], dkv[:, 1]], axis=1).reshape(512, 3, 4, 192)
    wqkv_g = dots("rpsc,rd->spcd", qkv_g, normed_one).astype(BF)
    ga = jnp.concatenate([wqkv_g, out_g[:, None]], axis=1)
    gm = jnp.stack([in_g, back_g], axis=1)
    col = jnp.sum(qkv_g.astype(F32), axis=0)
    first_grad = dots("rpsc,spcd->rd", qkv_g, wa[:, :3])
    first_gain_g = jnp.sum(first_grad * first_hat, axis=0)
    first_shift_g = jnp.sum(first_grad, axis=0)
    input_grad = mid_grad + norm_back(first_grad * first_gain, first_hat, first_inv)
    order = z ^ jnp.arange(4)
    pad = lambda v: jnp.pad(v, ((0, 0), (0, 576)))
    small = jnp.concatenate([
        jnp.take(in_bias_g, order, axis=0), jnp.take(pad(col[0]), order, axis=0), jnp.take(pad(col[2]), order, axis=0),
        first_gain_g[None], first_shift_g[None], second_gain_g[None], second_shift_g[None], out_bias_g[None], back_bias_g[None],
        jnp.zeros((6, 768), F32)])
    stays = c == z % 2
    seq_sum = jnp.zeros((8, 768), F32).at[0].set(jnp.sum(input_grad, axis=0))
    my_step = lax.all_gather(step.astype(F32), ("c", "mp"))
    src = jnp.where(stays, c * 4 + z, (1 - c) * 4 + (z ^ 1))
    seq_sum = seq_sum.at[1].set(my_step[src])
    outa, outm, small, seqs, input_grad, output = reduce_grads(ga, gm, small, seq_sum, input_grad, output)
    n_dh = lax.axis_size("dh")
    onehot = (jnp.arange(NSTEPS, dtype=jnp.int32)[:, None] == seqs[:, 1, 0].astype(jnp.int32)[None, :]).astype(F32)
    table = jnp.dot(onehot, seqs[:, 0], precision=HIGHEST)
    qkv_g = outa[:3].astype(F32)
    out_g = outa[3].astype(F32)
    in_g = outm[0].astype(F32)
    back_g = outm[1].astype(F32)
    if n_dh > 1:
        table, qkv_g, out_g, in_g, back_g, small = lax.psum((table, qkv_g, out_g, in_g, back_g, small), "dh")
    own = lambda first, n: lax.dynamic_index_in_dim(small[first:first + 4], z, keepdims=False)[:n]
    return (output, input_grad, table, qkv_g.transpose(2, 0, 1), jnp.stack([own(4, 192), own(8, 192)]), out_g, small[16],
            small[12], small[13], small[14], small[15], in_g, own(0, 768), back_g, small[17])


def solution(mesh):
    n_dp, n_mp = mesh.devices.shape
    fine = Mesh(mesh.devices.reshape(n_dp // 8, 4, 2, n_mp), ("dh", "k", "c", "mp"))
    dp = ("dh", "k", "c")
    rows = dp + ("mp",)
    in_specs = (P(rows, None), P(dp), P(rows), P(rows, None), P(), P(None, None, "mp"), P(None, "mp"), P("mp", None),
                P(), P(), P(), P(), P(), P(None, "mp"), P("mp"), P("mp", None), P())
    out_specs = (P(rows, None), P(rows, None), P(), P(None, None, "mp"), P(None, "mp"), P("mp", None), P(), P(), P(), P(), P(),
                 P(None, "mp"), P("mp"), P("mp", None), P())
    return jax.shard_map(shards, mesh=fine, in_specs=in_specs, out_specs=out_specs, check_vma=False)
```

```python
import functools

import jax
import jax.numpy as jnp
from jax import lax
from jax.experimental import pallas as pl
from jax.experimental.pallas import tpu as pltpu
from jax.sharding import Mesh, PartitionSpec as P

HEAD_DIM = 64
NSTEPS = 1000
L = 1024
EPSILON = 1e-05
HIGHEST = lax.Precision.HIGHEST
MESH = pl.DeviceIdType.MESH
BF = jnp.bfloat16
F32 = jnp.float32


def place():
    k = lax.axis_index("k")
    c = lax.axis_index("c")
    z = lax.axis_index("mp")
    return k, c, z


def flip(i, bit):
    if bit == 1:
        return i + 1 - 2 * lax.rem(i, 2)
    if bit == 2:
        return lax.rem(i + 2, 4)
    return 3 - i


def enter_barrier():
    k, c, z = place()
    sem = pltpu.get_barrier_semaphore()
    peers = [{"c": 1 - c}, {"k": flip(k, 1)}, {"k": flip(k, 2)}] + [{"mp": flip(z, r)} for r in (1, 2, 3)]
    peers.append({"c": 1 - c, "mp": flip(z, 1)})
    for peer in peers:
        pl.semaphore_signal(sem, inc=1, device_id=peer, device_id_type=MESH)
    pl.semaphore_wait(sem, len(peers))


def remote(src, dst, ss, rs, peer):
    return pltpu.make_async_remote_copy(src_ref=src, dst_ref=dst, send_sem=ss, recv_sem=rs, device_id=peer, device_id_type=MESH)


def cut(ref, lead, q, k, half, c):
    first, count = {None: (0, q), 0: (0, (q // 32) * 16 if q % 32 else q // 2), 1: ((q // 32) * 16 if q % 32 else q // 2, 0)}[half]
    if half == 1:
        count = q - first
    start = pl.multiple_of(k * q + first, 16)
    cols = pl.ds(pl.multiple_of(c * 384, 128), 384)
    return ref.at[lead + (slice(None), pl.ds(start, count), cols)]


def cols_of(ref, lead, c):
    return ref.at[lead + (slice(None), slice(None), pl.ds(pl.multiple_of(c * 384, 128), 384))]


def lane_mask(rows, j):
    lane = lax.broadcasted_iota(jnp.int32, (rows, 128), 1)
    return (lane < 64) if j == 0 else (lane >= 64)


def mm(a, b):
    return lax.dot_general(a, b, (((1,), (0,)), ((), ())), preferred_element_type=F32)


def mm_nt(a, b):
    return lax.dot_general(a, b, (((1,), (1,)), ((), ())), preferred_element_type=F32)


def norm_parts(values):
    center = values - jnp.mean(values, axis=-1, keepdims=True)
    inverse = lax.rsqrt(jnp.mean(center * center, axis=-1, keepdims=True) + EPSILON)
    return (center * inverse, inverse)


def norm_back(upstream, normal, inverse):
    return inverse * (
        upstream
        - jnp.mean(upstream, axis=-1, keepdims=True)
        - normal * jnp.mean(upstream * normal, axis=-1, keepdims=True)
    )


def col_sum(x):
    return jnp.sum(x, axis=0, keepdims=True)


def layer_kernel(qkv_ref, out_ref, in_ref, back_ref, bias_ref, tok_ref, grad_ref, row_ref, vec,
                 outa, outm, small_out, seq_out, ig_out, oo_out,
                 wa, wm, bias, tok, grad, row,
                 cra, crm, raa, rba, ram, rbm, bxa, bya, bxm, bym, za, zm, fa, fm, hyper, seq_buf,
                 gt, n1, q, kb, vb, att, lse, mid, acc, sg, n2, n2t, act, pg, br, dk_acc, dv_acc, dkt, dvt, dkr, dvr, igb,
                 local_sem, ssem, rsem, bsem, brem, wsem, wrem, kvs, kvr, dks, dkrs,
                 rss, rrs, fsem, frem, hsem, hrem, qsem, qrem, w2sem, w2rem):
    k, c, z = place()
    kx, ky, kd = flip(k, 1), flip(k, 2), flip(k, 3)
    nx, ny, nc = {"k": kx}, {"k": ky}, {"c": 1 - c}
    me = k * 8 + c * 4 + z
    every = slice(None)

    def start(cps):
        for cp in cps:
            cp.start()

    def got(cps):
        for cp in cps:
            cp.wait_recv()

    def sent(cps):
        for cp in cps:
            cp.wait_send()

    copies = [pltpu.make_async_copy(s, d, local_sem.at[i]) for i, (s, d) in enumerate([
        (qkv_ref, wa.at[0, pl.ds(0, 3)]),
        (out_ref, wa.at[0, 3]),
        (in_ref, wm.at[0, 0]),
        (back_ref, wm.at[0, 1]),
        (bias_ref, bias.at[0]),
    ])]
    start(copies)
    enter_barrier()
    stays = c == lax.rem(z, 2)
    moves = jnp.logical_not(stays)
    swap_peer = {"c": 1 - c, "mp": flip(z, 1)}

    def swap_start(remote_cps, local_cps):
        @pl.when(stays)
        def _():
            start(local_cps)

        @pl.when(moves)
        def _():
            start(remote_cps)

    def swap_wait(remote_cps, local_cps):
        @pl.when(stays)
        def _():
            for cp in local_cps:
                cp.wait()

        @pl.when(moves)
        def _():
            for cp in remote_cps:
                cp.wait()

    def swap_of(pairs, send, recv, first):
        return ([remote(s, d, send.at[i], recv.at[i], swap_peer) for i, (s, d) in enumerate(pairs)],
                [pltpu.make_async_copy(s, d, local_sem.at[first + i]) for i, (s, d) in enumerate(pairs)])

    swap_in = swap_of([(tok_ref, tok), (row_ref, row), (grad_ref, grad)], wsem, wrem, 5)
    for cp in copies[:2]:
        cp.wait()

    gchunks = [(wa, 48, 1), (wa, 48, 2), (wa, 48, 3), (wm, 192, 1), (wm, 192, 2), (wm, 192, 3)]
    ng = len(gchunks)

    def gsends(i):
        w, qr, r = gchunks[i]
        at = lambda slot, kk, half: cut(w, (slot,), qr, kk, half, c)
        return [
            [remote(at(0, k, None), at(r, k, None), ssem.at[i, 0], rsem.at[i, 0], {"mp": flip(z, r)})],
            [remote(at(r, k, None), at(r, k, None), ssem.at[i, 1], rsem.at[i, 1], nx),
             remote(at(r, k, None), at(r, k, None), ssem.at[i, 2], rsem.at[i, 2], ny)],
            [remote(at(r, ky, 0), at(r, ky, 0), ssem.at[i, 3], rsem.at[i, 3], nx),
             remote(at(r, kx, 1), at(r, kx, 1), ssem.at[i, 4], rsem.at[i, 4], ny)],
            [remote(cols_of(w, (r,), c), cols_of(w, (r,), c), ssem.at[i, 5], rsem.at[i, 5], nc)],
        ]

    def glands(i):
        w, qr, r = gchunks[i]
        at = lambda slot, kk, half: cut(w, (slot,), qr, kk, half, c)
        return [
            [(at(r, k, None), rsem.at[i, 0])],
            [(at(r, kx, None), rsem.at[i, 1]), (at(r, ky, None), rsem.at[i, 2])],
            [(at(r, kd, 0), rsem.at[i, 3]), (at(r, kd, 1), rsem.at[i, 4])],
            [(cols_of(w, (r,), 1 - c), rsem.at[i, 5])],
        ]

    g_sends = [gsends(i) for i in range(ng)]
    g_lands = [glands(i) for i in range(ng)]
    AHEAD = 2

    def gather_step(step):
        for stage in range(4):
            i = step - stage
            if 0 <= i < ng:
                for ref, sem in g_lands[i][stage]:
                    pltpu.make_async_copy(ref, ref, sem).wait()
                if stage == 0 and i + AHEAD < ng:
                    if i + AHEAD == 3:
                        for cp in copies[2:4]:
                            cp.wait()
                    start(g_sends[i + AHEAD][0])
                if stage < 3:
                    start(g_sends[i][stage + 1])

    small_cps = [remote(bias.at[0], bias.at[r], bsem.at[r - 1], brem.at[r - 1], {"mp": flip(z, r)}) for r in (1, 2, 3)]
    start(g_sends[0][0])
    copies[4].wait()
    start(small_cps)
    swap_start(*swap_in)
    start(g_sends[1][0])

    def ln_one():
        @pl.loop(0, 4)
        def _(i):
            r = pl.ds(pl.multiple_of(i * 128, 128), 128)
            hat, _inv = norm_parts(tok[r].astype(F32) + row[0:1].astype(F32))
            n1[r] = (hat * vec[0:1] + vec[1:2]).astype(BF)

    def transpose_into(dst, src, rows_n, cols0, cols_n):
        @pl.loop(0, rows_n // 128)
        def _(i):
            r = pl.ds(pl.multiple_of(i * 128, 128), 128)
            dst[pl.ds(cols0, cols_n), r] = jnp.transpose(src[r, pl.ds(cols0, cols_n)])

    def qkv_half(h):
        def one(p, dst, b):
            w = wa[2 * h:2 * h + 2, p].reshape(384, 768)

            @pl.loop(0, 2)
            def _(i):
                r = pl.ds(pl.multiple_of(i * 256, 256), 256)
                o = mm_nt(n1[r], w)
                if b is not None:
                    o = o + b
                dst[r, pl.ds(384 * h, 384)] = o.astype(BF)

        qb = bias[2 * h, 1:2, 0:384] + bias[2 * h + 1, 3:4, 0:384]
        vb_ = bias[2 * h, 2:3, 0:384] + bias[2 * h + 1, 4:5, 0:384]
        one(1, kb.at[c], None)
        one(2, vb.at[c], vb_)
        start(kv_cps[h])
        one(0, q, qb)

    half_cols = lambda ref, h: ref.at[every, pl.ds(384 * h, 384)]
    kv_cps = [[remote(half_cols(kb.at[c], h), half_cols(kb.at[c], h), kvs.at[h, 0], kvr.at[h, 0], nc),
               remote(half_cols(vb.at[c], h), half_cols(vb.at[c], h), kvs.at[h, 1], kvr.at[h, 1], nc)] for h in range(2)]

    def kv_wait(h):
        for j, b in enumerate((kb, vb)):
            pltpu.make_async_copy(half_cols(b.at[1 - c], h), half_cols(b.at[1 - c], h), kvr.at[h, j]).wait()

    QB = 256

    def attend(first, count):
        @pl.loop(0, count * (512 // QB))
        def _(n):
            t = first + n // (512 // QB)
            lanes = pl.ds(pl.multiple_of(t * 128, 128), 128)
            r = pl.ds(pl.multiple_of(lax.rem(n, 512 // QB) * QB, QB), QB)
            keys = kb[:, :, lanes].reshape(1024, 128)
            vals = vb[:, :, lanes].reshape(1024, 128)
            qs = q[r, lanes].astype(F32) * (HEAD_DIM ** -0.5)
            outs = []
            stats = lse[r]
            lane = lax.broadcasted_iota(jnp.int32, (QB, 128), 1)
            for j in range(2):
                s = mm_nt(jnp.where(lane_mask(QB, j), qs, 0.0).astype(BF), keys)
                peak = jnp.max(s, axis=-1, keepdims=True)
                e = jnp.exp(s - peak)
                total = jnp.sum(e, axis=-1, keepdims=True)
                o = mm(e.astype(BF), vals)
                outs.append(o / total)
                stats = jnp.where(lane == 2 * t + j, peak + jnp.log(total), stats)
            lse[r] = stats
            att[r, lanes] = jnp.where(lane_mask(QB, 0), outs[0], outs[1]).astype(BF)

    def out_and_norm():
        wo = wa[:, 3].reshape(768, 768)

        @pl.loop(0, 2)
        def _(i):
            r = pl.ds(pl.multiple_of(i * 256, 256), 256)
            m = (tok[r].astype(F32) + row[0:1].astype(F32)) + (mm(att[r], wo) + vec[4:5])
            mid[r] = m
            hat, _inv = norm_parts(m)
            n2[r] = (hat * vec[2:3] + vec[3:4]).astype(BF)

    C0 = 0.7978845608028654
    C1 = 0.044715

    def feed(r4):
        w_in = wm.at[r4, 0]
        w_back = wm.at[r4, 1]

        @pl.loop(0, 2)
        def _(i):
            r = pl.ds(pl.multiple_of(i * 256, 256), 256)
            u = mm(n2[r], w_in[...]) + bias[r4, 0:1]
            da = mm_nt(grad[r], w_back[...])
            uu = u * u
            th = jnp.tanh(u * (C0 + (C0 * C1) * uu))
            half = 0.5 * (1.0 + th)
            a = (u * half).astype(BF)
            slope = half + (0.5 * u) * (1.0 - th * th) * (C0 + (3.0 * C0 * C1) * uu)
            p = (da * slope).astype(BF)
            act[r] = a
            pg[r] = p
            f = mm(a, w_back[...])
            g2 = mm_nt(p, w_in[...])
            if r4 == 0:
                acc[r] = f
                sg[r] = g2
            else:
                acc[r] += f
                sg[r] += g2
        zr = flip2(z, r4)
        hyper[0, pl.ds(zr, 1)] = col_sum(pg[...].astype(F32))

    def feed_grads(r4):
        @pl.loop(0, 3)
        def _(i):
            r = pl.ds(pl.multiple_of(i * 256, 256), 256)
            wm[r4, 0, r] = mm(n2t[r], pg[...]).astype(BF)
            wm[r4, 1, r] = mm(gt[r], act[...]).astype(BF)

    def after_feed():
        zero = jnp.zeros((1, 768), F32)

        def body(i, sums):
            r = pl.ds(pl.multiple_of(i * 128, 128), 128)
            m = mid[r]
            n2[r] = (m + (acc[r] + vec[5:6])).astype(BF)
            hat, inv = norm_parts(m)
            g = sg[r]
            go = grad[r].astype(F32)
            mg = go + norm_back(g * vec[2:3], hat, inv)
            sg[r] = mg
            b = mg.astype(BF)
            br[r] = b
            return (sums[0] + col_sum(g * hat), sums[1] + col_sum(g), sums[2] + col_sum(b.astype(F32)), sums[3] + col_sum(go))

        sums = lax.fori_loop(0, 4, body, (zero,) * 4)
        hyper[0, 14:15] = sums[0]
        hyper[0, 15:16] = sums[1]
        hyper[0, 16:17] = sums[2]
        hyper[0, 17:18] = sums[3]

    def attended_back():
        wo = wa[:, 3].reshape(768, 768)

        @pl.loop(0, 2)
        def _(i):
            r = pl.ds(pl.multiple_of(i * 256, 256), 256)
            act[r] = mm_nt(br[r], wo).astype(BF)

    def out_grads():
        transpose_into(n2t, att, 512, 0, 768)
        for s in range(4):
            wa[s, 3] = mm(n2t[192 * s:192 * s + 192], br[...]).astype(BF)

    def attend_back(h):
        nq = 512 // QB

        @pl.loop(0, 3 * nq)
        def _(n):
            tt = n // nq
            t = 3 * h + tt
            i = lax.rem(n, nq)
            lanes = pl.ds(pl.multiple_of(t * 128, 128), 128)
            r = pl.ds(pl.multiple_of(i * QB, QB), QB)
            keys = kb[:, :, lanes].reshape(1024, 128)
            vals = vb[:, :, lanes].reshape(1024, 128)
            qs = q[r, lanes].astype(F32) * (HEAD_DIM ** -0.5)
            go = act[r, lanes].astype(F32)
            qs_t = jnp.transpose(qs).astype(BF)
            go_t = jnp.transpose(go).astype(BF)
            prod = go * att[r, lanes].astype(F32)
            stats = lse[r]
            lane = lax.broadcasted_iota(jnp.int32, (QB, 128), 1)
            dqs = []
            for j in range(2):
                mask = lane_mask(QB, j)
                s = mm_nt(jnp.where(mask, qs, 0.0).astype(BF), keys)
                le = jnp.sum(jnp.where(lane == 2 * t + j, stats, 0.0), axis=-1, keepdims=True)
                delta = jnp.sum(jnp.where(mask, prod, 0.0), axis=-1, keepdims=True)
                p = jnp.exp(s - le)
                dp = mm_nt(jnp.where(mask, go, 0.0).astype(BF), vals)
                ds = (p * (dp - delta)).astype(BF)
                dqs.append(mm(ds, keys))
                half = slice(64 * j, 64 * j + 64)
                dv = mm(go_t[half], p.astype(BF))
                dk = mm(qs_t[half], ds)

                @pl.when(i == 0)
                def _():
                    dv_acc[half] = dv
                    dk_acc[half] = dk

                @pl.when(i > 0)
                def _():
                    dv_acc[half] += dv
                    dk_acc[half] += dk
            dq = jnp.where(lane_mask(QB, 0), dqs[0], dqs[1]) * (HEAD_DIM ** -0.5)
            pg[r, lanes] = dq.astype(BF)

            @pl.when(i == nq - 1)
            def _():
                dkt[:, lanes_to_rows(t)] = jnp.stack([dk_acc[:, 0:512], dk_acc[:, 512:1024]]).astype(BF)
                dvt[:, lanes_to_rows(t)] = jnp.stack([dv_acc[:, 0:512], dv_acc[:, 512:1024]]).astype(BF)

        start(dkv_cps[h])

    lanes_to_rows = lambda t: pl.ds(pl.multiple_of(t * 128, 128), 128)
    rows_half = lambda ref, h: ref.at[pl.ds(384 * h, 384)]
    dkv_cps = [[remote(rows_half(dkt.at[1 - c], h), rows_half(dkr, h), dks.at[h, 0], dkrs.at[h, 0], nc),
                remote(rows_half(dvt.at[1 - c], h), rows_half(dvr, h), dks.at[h, 1], dkrs.at[h, 1], nc)] for h in range(2)]

    def qkv_back(h):
        got(dkv_cps[h])
        cols = pl.ds(384 * h, 384)
        transpose_into(gt, pg, 512, 384 * h, 384)

        @pl.loop(0, 3)
        def _(i):
            rr = pl.ds(pl.multiple_of(384 * h + i * 128, 128), 128)
            dkf = (dkt[c, rr].astype(F32) + dkr[rr].astype(F32)).astype(BF)
            dvf = (dvt[c, rr].astype(F32) + dvr[rr].astype(F32)).astype(BF)
            dkr[rr] = dkf
            dvr[rr] = dvf
            att[:, rr] = jnp.transpose(dkf)
            act[:, rr] = jnp.transpose(dvf)
        ws = [wa[2 * h:2 * h + 2, p].reshape(384, 768) for p in range(3)]

        @pl.loop(0, 2)
        def _(i):
            r = pl.ds(pl.multiple_of(i * 256, 256), 256)
            f = mm(pg[r, cols], ws[0]) + mm(att[r, cols], ws[1]) + mm(act[r, cols], ws[2])
            if h == 0:
                acc[r] = f
            else:
                acc[r] += f
        sums = (col_sum(pg[:, cols].astype(F32)), col_sum(act[:, cols].astype(F32)))
        lane = lax.broadcasted_iota(jnp.int32, (1, 384), 1)
        for j in range(2):
            zr = flip2(z, 2 * h + j)
            keep = (lane < 192) if j == 0 else (lane >= 192)
            for b, v in ((4, sums[0]), (8, sums[1])):
                hyper[0, pl.ds(b + zr, 1), 0:384] = jnp.where(keep, v, 0.0)
        for s in (2 * h, 2 * h + 1):
            rr = pl.ds(192 * s, 192)
            wa[s, 0] = mm(gt[rr], n1[...]).astype(BF)
            wa[s, 1] = mm(dkr[rr], n1[...]).astype(BF)
            wa[s, 2] = mm(dvr[rr], n1[...]).astype(BF)

    def last_norm():
        zero = jnp.zeros((1, 768), F32)

        def body(i, sums):
            r = pl.ds(pl.multiple_of(i * 128, 128), 128)
            hat, inv = norm_parts(tok[r].astype(F32) + row[0:1].astype(F32))
            g = acc[r]
            ig = sg[r] + norm_back(g * vec[0:1], hat, inv)
            igb[r] = ig.astype(BF)
            return (sums[0] + col_sum(g * hat), sums[1] + col_sum(g), sums[2] + col_sum(ig))

        sums = lax.fori_loop(0, 4, body, (zero,) * 3)
        hyper[0, 12:13] = sums[0]
        hyper[0, 13:14] = sums[1]
        seq_buf[pl.ds(me, 1), 0:1] = sums[2][None]
        step = row[1:2].astype(F32) * 32.0 + row[2:3].astype(F32)
        seq_buf[pl.ds(me, 1), 1:2] = step[None]

    chunks = [(wm, crm, r, 1, 192, ram, rbm, bxm, bym, zm) for r in range(4)]
    chunks += [(wa, cra, 2 * h, 2, 48, raa, rba, bxa, bya, za) for h in range(2)]
    mine = pl.ds(pl.multiple_of(c * 384, 128), 384)
    other = pl.ds(pl.multiple_of((1 - c) * 384, 128), 384)

    def rows(qr, kk, half):
        first = (qr // 32) * 16 if qr % 32 else qr // 2
        first, count = (0, qr) if half is None else ((0, first) if half == 0 else (first, qr - first))
        return pl.ds(pl.multiple_of(kk * qr + first, 16), count)

    def make(i):
        g, cr, s0, ns, qr, ra, rb, bx, by, zz = chunks[i]
        ss = pl.ds(s0, ns)
        return [
            [remote(g.at[ss, every, every, other], cr.at[ss], rss.at[i, 0], rrs.at[i, 0], nc)],
            [remote(g.at[ss, every, rows(qr, kd, 0), mine], ra.at[ss], rss.at[i, 1], rrs.at[i, 1], nx),
             remote(g.at[ss, every, rows(qr, kd, 1), mine], rb.at[ss], rss.at[i, 2], rrs.at[i, 2], ny)],
            [remote(g.at[ss, every, rows(qr, kx, None), mine], bx.at[ss], rss.at[i, 3], rrs.at[i, 3], nx),
             remote(g.at[ss, every, rows(qr, ky, None), mine], by.at[ss], rss.at[i, 4], rrs.at[i, 4], ny)],
            [remote(g.at[r, every, rows(qr, k, None), mine], zz.at[r - 1], rss.at[i, 4 + r], rrs.at[i, 4 + r], {"mp": flip(z, r)})
             for r in range(max(s0, 1), s0 + ns)],
        ]

    r_sends = [make(i) for i in range(len(chunks))]

    def add_into(dst, pieces):
        n, m = dst.shape[0], dst.shape[1]
        for a in range(n):
            for b in range(m):
                total = dst[a, b].astype(F32)
                for p in pieces:
                    total = total + p[a, b].astype(F32)
                dst[a, b] = total.astype(BF)

    def core_add(i):
        g, cr, s0, ns, qr, *_ = chunks[i]

        @pl.loop(0, 4)
        def _(j):
            r = pl.ds(pl.multiple_of(j * qr, 16), qr)
            add_into(g.at[pl.ds(s0, ns), :, r, mine], [cr.at[pl.ds(s0, ns), :, r]])

    def a_add(i):
        g, cr, s0, ns, qr, ra, rb, *_ = chunks[i]
        ss = pl.ds(s0, ns)
        add_into(g.at[ss, :, rows(qr, ky, 0), mine], [ra.at[ss]])
        add_into(g.at[ss, :, rows(qr, kx, 1), mine], [rb.at[ss]])

    def b_add(i):
        g, cr, s0, ns, qr, ra, rb, bx, by, zz = chunks[i]
        ss = pl.ds(s0, ns)
        add_into(g.at[ss, :, rows(qr, k, None), mine], [bx.at[ss], by.at[ss]])

    adds = [None, core_add, a_add, b_add]

    def reduce_stage(i, stage):
        if stage > 0:
            got(r_sends[i][stage - 1])
        if stage < 4:
            if stage > 0:
                adds[stage](i)
            start(r_sends[i][stage])

    finals = [(wm, zm, fm, 192, 0), (wa, za, fa, 48, 1)]

    def final_sends(j):
        g, zz, f, qr, _ = finals[j]
        at = lambda kk, half: f.at[:, rows(qr, kk, half), mine]
        return [
            [remote(at(k, None), at(k, None), fsem.at[j, 0], frem.at[j, 0], nx),
             remote(at(k, None), at(k, None), fsem.at[j, 1], frem.at[j, 1], ny)],
            [remote(at(ky, 0), at(ky, 0), fsem.at[j, 2], frem.at[j, 2], nx),
             remote(at(kx, 1), at(kx, 1), fsem.at[j, 3], frem.at[j, 3], ny)],
            [remote(f.at[:, :, mine], f.at[:, :, mine], fsem.at[j, 4], frem.at[j, 4], nc)],
        ]

    f_sends = [final_sends(j) for j in range(2)]

    def final_sum(j):
        g, zz, f, qr, _ = finals[j]
        for b in range(g.shape[1]):
            total = g[0, b, rows(qr, k, None), mine].astype(F32)
            for r in range(3):
                total = total + zz[r, b].astype(F32)
            f[b, rows(qr, k, None), mine] = total.astype(BF)
        start(f_sends[j][0])

    def final_stage(j, stage):
        got(f_sends[j][stage - 1])
        if stage < 3:
            start(f_sends[j][stage])

    hyper[0] = jnp.zeros(hyper.shape[1:], F32)
    seq_buf[pl.ds(me, 1)] = jnp.zeros((1, 8, 768), F32)
    lse[...] = jnp.zeros_like(lse)
    gather_step(0)
    swap_wait(*swap_in)
    ln_one()
    transpose_into(gt, grad, 512, 0, 768)
    gather_step(1)
    for cp in small_cps:
        cp.wait()
    gather_step(2)
    gather_step(3)
    qkv_half(0)
    gather_step(4)
    kv_wait(0)
    attend(0, 3)
    gather_step(5)
    qkv_half(1)
    gather_step(6)
    kv_wait(1)
    attend(3, 3)
    out_and_norm()
    transpose_into(n2t, n2, 512, 0, 768)
    gather_step(7)
    feed(0)
    gather_step(8)
    for i in range(ng):
        for stage in range(4):
            sent(g_sends[i][stage])
    feed_grads(0)
    reduce_stage(0, 0)
    feed(1)
    reduce_stage(0, 1)
    feed_grads(1)
    reduce_stage(1, 0)
    reduce_stage(0, 2)
    feed(2)
    reduce_stage(1, 1)
    reduce_stage(0, 3)
    feed_grads(2)
    reduce_stage(2, 0)
    reduce_stage(1, 2)
    feed(3)
    reduce_stage(0, 4)
    reduce_stage(2, 1)
    reduce_stage(1, 3)
    feed_grads(3)
    reduce_stage(3, 0)
    reduce_stage(2, 2)
    after_feed()
    swap_out = swap_of([(n2, oo_out)], w2sem, w2rem, 8)
    swap_start(*swap_out)
    reduce_stage(1, 4)
    reduce_stage(3, 1)
    reduce_stage(2, 3)
    attended_back()
    out_grads()
    reduce_stage(3, 2)
    attend_back(0)
    reduce_stage(2, 4)
    reduce_stage(3, 3)
    attend_back(1)
    sent(kv_cps[0] + kv_cps[1])
    reduce_stage(3, 4)
    final_sum(0)
    qkv_back(0)
    reduce_stage(4, 0)
    final_stage(0, 1)
    qkv_back(1)
    reduce_stage(5, 0)
    final_stage(0, 2)
    reduce_stage(4, 1)
    last_norm()
    swap_ig = ([remote(igb, ig_out, w2sem.at[1], w2rem.at[1], swap_peer)], [pltpu.make_async_copy(igb, ig_out, local_sem.at[9])])
    swap_start(*swap_ig)
    reduce_stage(5, 1)
    final_stage(0, 3)
    out_m = pltpu.make_async_copy(fm, outm, local_sem.at[10])
    out_m.start()
    peers = [nc, nx, ny, {"mp": flip(z, 1)}, {"mp": flip(z, 2)}]
    hops = [remote(hyper.at[2 * t], hyper.at[2 * t + 1], hsem.at[t], hrem.at[t], peer) for t, peer in enumerate(peers)]

    def hop(t):
        got([hops[t]])
        hyper[2 * t + 2] = hyper[2 * t] + hyper[2 * t + 1]
        if t < 4:
            start([hops[t + 1]])

    mine_seq = seq_buf.at[pl.ds(me, 1)]
    zq = lambda kk, cc, zz_: seq_buf.at[pl.ds(kk * 8 + cc * 4 + zz_, 1)]
    line = lambda kk, cc: seq_buf.at[pl.ds(kk * 8 + cc * 4, 4)]
    chip = lambda kk: seq_buf.at[pl.ds(kk * 8, 8)]
    q_sends = [
        [remote(mine_seq, mine_seq, qsem.at[r - 1], qrem.at[r - 1], {"mp": flip(z, r)}) for r in (1, 2, 3)],
        [remote(line(k, c), line(k, c), qsem.at[3], qrem.at[3], nc)],
        [remote(chip(k), chip(k), qsem.at[4], qrem.at[4], nx), remote(chip(k), chip(k), qsem.at[5], qrem.at[5], ny)],
        [remote(chip(ky), chip(ky), qsem.at[6], qrem.at[6], nx)],
    ]
    start(q_sends[0])
    start([hops[0]])
    reduce_stage(4, 2)
    hop(0)
    reduce_stage(5, 2)
    got(q_sends[0])
    start(q_sends[1])
    hop(1)
    reduce_stage(4, 3)
    got(q_sends[1])
    start(q_sends[2])
    reduce_stage(5, 3)
    hop(2)
    got(q_sends[2])
    start(q_sends[3])
    reduce_stage(4, 4)
    reduce_stage(5, 4)
    final_sum(1)
    hop(3)
    final_stage(1, 1)
    hop(4)
    small_cp = pltpu.make_async_copy(hyper.at[10], small_out, local_sem.at[11])
    small_cp.start()
    final_stage(1, 2)
    got(q_sends[3])
    seq_cp = pltpu.make_async_copy(seq_buf, seq_out, local_sem.at[12])
    seq_cp.start()
    final_stage(1, 3)
    out_a = pltpu.make_async_copy(fa, outa, local_sem.at[13])
    out_a.start()
    for st in r_sends + f_sends + q_sends_list(q_sends):
        for cps in st:
            sent(cps)
    sent(hops)
    sent(dkv_cps[0] + dkv_cps[1])
    swap_wait(*swap_out)
    swap_wait(*swap_ig)
    for cp in (out_m, small_cp, seq_cp, out_a):
        cp.wait()


def q_sends_list(q_sends):
    return [q_sends]


def flip2(z, r):
    return z if r == 0 else flip(z, r)


def layer(qkv, out, win, back, bias, tok, grad, row, vec):
    hbm = pl.BlockSpec(memory_space=pl.ANY)
    dma = pltpu.SemaphoreType.DMA
    vm = pltpu.VMEM
    shapes = (
        jax.ShapeDtypeStruct((4, 192, 768), BF),
        jax.ShapeDtypeStruct((2, 768, 768), BF),
        jax.ShapeDtypeStruct((24, 768), F32),
        jax.ShapeDtypeStruct((32, 8, 768), F32),
        jax.ShapeDtypeStruct((512, 768), BF),
        jax.ShapeDtypeStruct((512, 768), BF),
    )
    rows16 = vm((512, 768), BF)
    rows32 = vm((512, 768), F32)
    scratch = [
        vm((4, 4, 192, 768), BF), vm((4, 2, 768, 768), BF), vm((4, 8, 768), F32), rows16, rows16, vm((16, 768), BF),
        vm((4, 4, 192, 384), BF), vm((4, 2, 768, 384), BF),
        vm((4, 4, 16, 384), BF), vm((4, 4, 32, 384), BF), vm((4, 2, 96, 384), BF), vm((4, 2, 96, 384), BF),
        vm((4, 4, 48, 384), BF), vm((4, 4, 48, 384), BF), vm((4, 2, 192, 384), BF), vm((4, 2, 192, 384), BF),
        vm((3, 4, 48, 384), BF), vm((3, 2, 192, 384), BF), vm((4, 192, 768), BF), vm((2, 768, 768), BF),
        vm((11, 24, 768), F32), vm((32, 8, 768), F32),
        vm((768, 512), BF), rows16, rows16, vm((2, 512, 768), BF), vm((2, 512, 768), BF), rows16, vm((512, 128), F32),
        rows32, rows32, rows32, rows16, vm((768, 512), BF), rows16, rows16, rows16,
        vm((128, 1024), F32), vm((128, 1024), F32), vm((2, 768, 512), BF), vm((2, 768, 512), BF), vm((768, 512), BF), vm((768, 512), BF),
        rows16,
        dma((14,)), dma((6, 6)), dma((6, 6)), dma((3,)), dma((3,)), dma((3,)), dma((3,)),
        dma((2, 2)), dma((2, 2)), dma((2, 2)), dma((2, 2)),
        dma((6, 8)), dma((6, 8)), dma((2, 5)), dma((2, 5)), dma((5,)), dma((5,)), dma((7,)), dma((7,)), dma((2,)), dma((2,)),
    ]
    return pl.pallas_call(
        layer_kernel,
        out_shape=shapes,
        in_specs=[hbm] * 8 + [pl.BlockSpec(memory_space=pltpu.VMEM)],
        out_specs=[hbm] * 6,
        scratch_shapes=scratch,
        compiler_params=pltpu.CompilerParams(collective_id=0, has_side_effects=True, vmem_limit_bytes=63 << 20),
        name="layer",
    )(qkv, out, win, back, bias, tok, grad, row, vec)


def shards(tokens, timesteps, masked, cotangent, step_table, qkv_weight, qv_bias, out_weight, out_bias,
           first_gain, first_shift, second_gain, second_shift, in_weight, in_bias, back_weight, back_bias):
    z = lax.axis_index("mp")
    step = lax.dynamic_index_in_dim(timesteps, z // 2, keepdims=False)
    row = lax.dynamic_slice_in_dim(step_table, step, 1, axis=0)
    parts = jnp.stack([step // 32, step % 32]).astype(BF)
    row16 = jnp.concatenate([row, jnp.broadcast_to(parts[:, None], (2, 768)), jnp.zeros((13, 768), BF)])
    grad_low = cotangent * masked.astype(BF)[:, None]
    low_lanes = jnp.pad(qv_bias, ((0, 0), (0, 576)))
    high_lanes = jnp.pad(qv_bias, ((0, 0), (192, 384)))
    bias = jnp.concatenate([in_bias.astype(F32)[None], low_lanes, high_lanes, jnp.zeros((3, 768), F32)])
    vec = jnp.stack([first_gain, first_shift, second_gain, second_shift, out_bias, back_bias, out_bias, out_bias])
    outa, outm, small, seqs, input_grad, output = layer(
        qkv_weight.transpose(1, 2, 0), out_weight, in_weight, back_weight, bias, tokens, grad_low, row16, vec)
    onehot = (jnp.arange(NSTEPS, dtype=jnp.int32)[:, None] == seqs[:, 1, 0].astype(jnp.int32)[None, :]).astype(F32)
    table = jnp.dot(onehot, seqs[:, 0], precision=HIGHEST)
    qkv_g = outa[:3].astype(F32)
    out_g = outa[3].astype(F32)
    in_g = outm[0].astype(F32)
    back_g = outm[1].astype(F32).T
    if lax.axis_size("dh") > 1:
        table, qkv_g, out_g, in_g, back_g, small = lax.psum((table, qkv_g, out_g, in_g, back_g, small), "dh")
    own = lambda first: lax.dynamic_index_in_dim(small[first:first + 4], z, keepdims=False)
    qv_g = jnp.stack([own(4)[:192] + own(4)[192:384], own(8)[:192] + own(8)[192:384]])
    return (output, input_grad.astype(F32), table, qkv_g.transpose(2, 0, 1), qv_g, out_g, small[16],
            small[12], small[13], small[14], small[15], in_g, own(0), back_g, small[17])


def solution(mesh):
    n_dp, n_mp = mesh.devices.shape
    fine = Mesh(mesh.devices.reshape(n_dp // 8, 4, 2, n_mp), ("dh", "k", "c", "mp"))
    dp = ("dh", "k", "c")
    rows = dp + ("mp",)
    in_specs = (P(rows, None), P(dp), P(rows), P(rows, None), P(), P(None, None, "mp"), P(None, "mp"), P("mp", None),
                P(), P(), P(), P(), P(), P(None, "mp"), P("mp"), P("mp", None), P())
    out_specs = (P(rows, None), P(rows, None), P(), P(None, None, "mp"), P(None, "mp"), P("mp", None), P(), P(), P(), P(), P(),
                 P(None, "mp"), P("mp"), P("mp", None), P())
    return jax.shard_map(shards, mesh=fine, in_specs=in_specs, out_specs=out_specs, check_vma=False)
```
